32 devices in a mesh: rows: 4 (over x, core), cols: 8 (over z, y).
Axes of the slice: x: 2, y: 2, z: 4, core: 2. Of those that a mesh axis runs over, the one named last changes fastest.
Arguments:
- tensor: float32 [48, 256, 512], P('rows', 'cols'), may hold values from 0 to 1
- first_factor: float32 [48, 256], P('rows', 'cols'), may hold values from -2.5 to 2.5
- second_factor: float32 [256, 256], P('cols', 'rows'), may hold values from -2.5 to 2.5
- third_factor: float32 [512, 256], P(('rows', 'cols')), may hold values from -2.5 to 2.5
Outputs:
- first_new: float32 [48, 256], P('rows', 'cols')
- second_new: float32 [256, 256], P('cols', 'rows')
- third_new: float32 [512, 256], P(('rows', 'cols'))
The draws below stay inside these ranges and needn't reach their ends.
All inputs are finite; a program needn't handle non-finite values.
Results may differ from the reference program's by a relative error of at most 0.0003.
Values sent between devices are 32-bit elements; how exact they have to be, the bound alone decides.
A program may use at most 64 MiB of HBM per device.

```python
import jax
import jax.numpy as jnp
from jax import lax

RANK = 256
K = 512
I_DEV = 12
J_DEV = 32
STEPS = 2
I = 48
J = 256
N_ROWS = 4
N_COLS = 8


def shard_levels(own_key, shape, shards, least, high):
    def one(position, parts):
        draws = jax.random.uniform(jax.random.fold_in(jax.random.fold_in(own_key, 6), position), (parts,), jnp.float32, least / len(shards), high / len(shards))
        return jnp.repeat(jnp.exp(draws), shape[position] // parts).reshape((-1,) + (1,) * (len(shape) - position - 1))

    level = one(*shards[0])
    for cut in shards[1:]:
        level = level * one(*cut)
    return level


def noise(key, extent, deviation, limit, shards=(), kind=jnp.bfloat16):
    values = deviation * jax.random.normal(key, extent, jnp.float32)
    if shards:
        values = values * shard_levels(key, extent, shards, -0.22, 0.18)
    return jnp.clip(values, -limit, limit).astype(kind)


def setup_inputs(seed: int = 0) -> dict:
    splits = jax.random.split(jax.random.key(seed), 5)
    return {
        "tensor": jnp.clip(1.0 * jax.random.uniform(splits[0], (I, J, K), jnp.float32) ** shard_levels(splits[0], (I, J, K), ((0, 4), (1, 8)), -0.2, 0.2), 0.0, 1.0),
        "first_factor": noise(splits[1], (I, RANK), 0.4, 2.5, ((0, 4), (1, 8)), jnp.float32),
        "second_factor": noise(splits[2], (J, RANK), 0.4, 2.5, ((0, 8), (1, 4)), jnp.float32),
        "third_factor": noise(splits[3], (K, RANK), 0.4, 2.5, ((0, 32),), jnp.float32),
    }


def reference(tensor, first_factor, second_factor, third_factor):
    high = lax.Precision.HIGHEST
    size_i = I_DEV * N_ROWS
    size_j = J_DEV * N_COLS
    blocks = tensor.reshape(N_ROWS, I_DEV, size_j, K)
    factor_a, factor_b, factor_c = (first_factor, second_factor, third_factor)
    for step_index in range(STEPS):

        def one_block(carry, inputs):
            grad_b, grad_c = carry
            tile, rows_a = inputs
            khatri = (rows_a[:, None, :] * factor_b[None, :, :]).reshape(-1, RANK)
            model_tile = jnp.dot(khatri, factor_c.T, precision=high, preferred_element_type=jnp.float32)
            deriv = jax.nn.sigmoid(model_tile) - tile.reshape(-1, K)
            deriv_c = jnp.dot(deriv, factor_c, precision=high, preferred_element_type=jnp.float32).reshape(I_DEV, size_j, RANK)
            grad_a = jnp.einsum('ijr,jr->ir', deriv_c, factor_b, precision=high)
            grad_b = grad_b + jnp.einsum('ijr,ir->jr', deriv_c, rows_a, precision=high)
            grad_c = grad_c + lax.dot_general(deriv, khatri, (((0,), (0,)), ((), ())), precision=high, preferred_element_type=jnp.float32)
            return ((grad_b, grad_c), grad_a)
        start = (jnp.zeros((size_j, RANK), jnp.float32), jnp.zeros((K, RANK), jnp.float32))
        (grad_b, grad_c), grad_a = lax.scan(one_block, start, (blocks, factor_a.reshape(N_ROWS, I_DEV, RANK)))
        grad_a = grad_a.reshape(size_i, RANK)
        factor_a = factor_a - 4.0 / jnp.sqrt(jnp.float32(size_j * K)) * grad_a
        factor_b = factor_b - 4.0 / jnp.sqrt(jnp.float32(size_i * K)) * grad_b
        factor_c = factor_c - 4.0 / jnp.sqrt(jnp.float32(size_i * size_j)) * grad_c
    return (factor_a, factor_b, factor_c)
```

```python
import functools

import jax
import jax.numpy as jnp
from jax import lax
from jax.experimental import pallas as pl
from jax.experimental.pallas import tpu as pltpu
from jax.sharding import PartitionSpec as P

STEPS = 2
MESH = pl.DeviceIdType.MESH


def gather_third(piece):
    return lax.all_gather(piece, ("rows", "cols"), axis=0, tiled=True)


def plain_steps(tensor, first_factor, second_factor, third_factor):
    high = lax.Precision.HIGHEST
    rows_dev, cols_dev, depth = tensor.shape
    rate_a, rate_b, rate_c = rates(tensor)
    flat_target = tensor.reshape(-1, depth)
    shard_a, shard_b = (first_factor, second_factor)
    whole_c = gather_third(third_factor)
    for step_index in range(STEPS):
        whole_a = lax.all_gather(shard_a, "cols", axis=1, tiled=True)
        whole_b = lax.all_gather(shard_b, "rows", axis=1, tiled=True)
        khatri = (whole_a[:, None, :] * whole_b[None, :, :]).reshape(-1, whole_a.shape[1])
        model_tile = jnp.dot(khatri, whole_c.T, precision=high, preferred_element_type=jnp.float32)
        deriv = jax.nn.sigmoid(model_tile) - flat_target
        deriv_c = jnp.dot(
            deriv, whole_c, precision=high, preferred_element_type=jnp.float32
        ).reshape(rows_dev, cols_dev, -1)
        term_a = jnp.einsum("ijr,jr->ir", deriv_c, whole_b, precision=high)
        term_b = jnp.einsum("ijr,ir->jr", deriv_c, whole_a, precision=high)
        term_c = lax.dot_general(
            deriv, khatri, (((0,), (0,)), ((), ())), precision=high,
            preferred_element_type=jnp.float32,
        )
        shard_a = shard_a - rate_a * lax.psum_scatter(
            term_a, "cols", scatter_dimension=1, tiled=True
        )
        shard_b = shard_b - rate_b * lax.psum_scatter(
            term_b, "rows", scatter_dimension=1, tiled=True
        )
        whole_c = whole_c - rate_c * lax.psum(term_c, ("rows", "cols"))
    owner = lax.axis_index("rows") * lax.axis_size("cols") + lax.axis_index("cols")
    count = third_factor.shape[0]
    shard_c = lax.dynamic_slice_in_dim(whole_c, owner * count, count, 0)
    return (shard_a, shard_b, shard_c)


def rates(tensor):
    rows_dev, cols_dev, depth = tensor.shape
    size_i = rows_dev * lax.axis_size("rows")
    size_j = cols_dev * lax.axis_size("cols")
    return (
        4.0 / float(size_j * depth) ** 0.5,
        4.0 / float(size_i * depth) ** 0.5,
        4.0 / float(size_i * size_j) ** 0.5,
    )


def split(x):
    hi = x.astype(jnp.bfloat16)
    return hi, (x - hi.astype(jnp.float32)).astype(jnp.bfloat16)


def dot3(lhs, rhs, dims):
    def one(a, b):
        return lax.dot_general(a, b, (dims, ((), ())), preferred_element_type=jnp.float32)

    return one(lhs[0], rhs[0]) + (one(lhs[0], rhs[1]) + one(lhs[1], rhs[0]))


def kernel(
    n_rows, n_cols, rate, target_ref, a_ref, b_ref, c_ref, a_out, b_out, c_out,
    a_slots, b_slots, c_whole, c_term, from_core, to_x, from_x, to_col, from_col,
    khatri_hi, khatri_lo, deriv_hi, deriv_lo, place_a, place_b, send_sem, recv_sem,
):
    half = n_rows // 2
    n_i, n_j = a_ref.shape[0], b_ref.shape[0]
    width_a, width_b = a_ref.shape[1], b_ref.shape[1]
    rank = c_ref.shape[1]
    row, col = lax.axis_index("rows"), lax.axis_index("cols")
    plane, core = lax.div(row, 2), lax.rem(row, 2)
    other = 1 - core
    used = []

    def turn(base, offset, size):
        return lax.rem(base + offset, size)

    def send(src, dst, to_row, to_col_index):
        number = len(used)
        copy = pltpu.make_async_remote_copy(
            src_ref=src, dst_ref=dst, send_sem=send_sem.at[number], recv_sem=recv_sem.at[number],
            device_id=(to_row, to_col_index), device_id_type=MESH,
        )
        used.append(copy)
        copy.start()
        return copy

    barrier = pltpu.get_barrier_semaphore()
    for k in range(1, n_cols):
        pl.semaphore_signal(barrier, inc=1, device_id=(row, turn(col, k, n_cols)), device_id_type=MESH)
    for k in range(1, n_rows):
        pl.semaphore_signal(barrier, inc=1, device_id=(turn(row, k, n_rows), col), device_id_type=MESH)
    pl.semaphore_wait(barrier, n_cols + n_rows - 2)

    def share_first(version):
        return [
            send(a_slots.at[version, col], a_slots.at[version, col], row, turn(col, k, n_cols))
            for k in range(1, n_cols)
        ]

    def share_second(version):
        return [
            send(b_slots.at[version, row], b_slots.at[version, row], turn(row, k, n_rows), col)
            for k in range(1, n_rows)
        ]

    def total(slots, version, copies):
        for copy in copies:
            copy.wait_recv()
        result = slots[version, 0]
        for k in range(1, slots.shape[1]):
            result = result + slots[version, k]
        return result

    def gather_start(version, src):
        return [
            send(src, c_whole.at[version, plane, core, col], row, turn(col, k, n_cols))
            for k in range(1, n_cols)
        ]

    def gather_finish(version, copies):
        whole = c_whole.at[version]
        across, partner = [], []
        for k in range(n_cols):
            place = turn(col, n_cols - k, n_cols)
            if k:
                copies[k - 1].wait_recv()
            piece = whole.at[plane, core, place]
            across.append([
                send(piece, piece, turn(plane, h, half) * 2 + core, col) for h in range(1, half)
            ])
            partner.append(send(piece, piece, plane * 2 + other, col))
        for k in range(n_cols):
            place = turn(col, n_cols - k, n_cols)
            for h in range(1, half):
                across[k][h - 1].wait_recv()
                piece = whole.at[turn(plane, half - h, half), core, place]
                partner.append(send(piece, piece, plane * 2 + other, col))
        for copy in partner:
            copy.wait_recv()

    begun = gather_start(0, c_ref)
    c_whole[0, plane, core, col] = c_ref[...]
    place_a[...] = jnp.zeros_like(place_a)
    place_a[:n_i, :width_a] = a_ref[...]
    a_slots[0, col] = pltpu.roll(place_a[...], col * width_a, 1)
    place_b[...] = jnp.zeros_like(place_b)
    place_b[:, :width_b] = b_ref[...]
    b_slots[0, row] = pltpu.roll(place_b[...], row * width_b, 1)
    sent_a, sent_b = share_first(0), share_second(0)
    c_shard = c_ref[...]
    a_full = total(a_slots, 0, sent_a)
    b_full = total(b_slots, 0, sent_b)

    for step in range(STEPS):
        last = step == STEPS - 1
        for i in range(n_i):
            rows_here = pl.ds(i * n_j, n_j)
            hi, lo = split(a_full[i : i + 1, :] * b_full)
            khatri_hi[rows_here, :] = hi
            khatri_lo[rows_here, :] = lo
        gather_finish(step, begun)
        khatri = khatri_hi[...], khatri_lo[...]
        c_parts = split(c_whole[step].reshape(-1, rank))
        model = dot3(khatri, c_parts, ((1,), (1,)))
        deriv = split(jax.nn.sigmoid(model) - target_ref[...])
        deriv_hi[...], deriv_lo[...] = deriv
        term = c_term.at[step]
        term[...] = dot3(deriv, khatri, ((0,), (0,))).reshape(term.shape)
        order = [(h, turn(plane, h, half)) for h in list(range(1, half)) + [0]]
        core_copies = [
            send(term.at[there, other], from_core.at[step, there], plane * 2 + other, col)
            for _, there in order
        ]
        deriv_c = dot3((deriv_hi[...], deriv_lo[...]), c_parts, ((1,), (0,)))
        deriv_c = deriv_c.reshape(n_i, n_j, rank)
        x_copies = []
        for (h, there), copy in zip(order[:-1], core_copies[:-1]):
            copy.wait_recv()
            for k in range(n_cols):
                place = turn(col, k, n_cols)
                to_x[step, h - 1, k] = term[there, core, place] + from_core[step, there, place]
                x_copies.append(
                    send(to_x.at[step, h - 1, k], from_x.at[step, h - 1, k], there * 2 + core, col)
                )
        grad_b = jnp.sum(deriv_c * a_full[:n_i, None, :], axis=0)
        b_slots[step + 1, row] = grad_b
        sent_b = share_second(step + 1)
        grad_a = jnp.sum(deriv_c * b_full[None, :, :], axis=1)
        a_slots[step + 1, col] = jnp.zeros_like(place_a)
        a_slots[step + 1, col, :n_i, :] = grad_a
        sent_a = share_first(step + 1)
        core_copies[-1].wait_recv()
        col_copies = []
        for k in list(range(1, n_cols)) + [0]:
            place = turn(col, k, n_cols)
            piece = term[plane, core, place] + from_core[step, plane, place]
            for h in range(1, half):
                x_copies[(h - 1) * n_cols + k].wait_recv()
                piece = piece + from_x[step, h - 1, k]
            if k:
                to_col[step, k - 1] = piece
                col_copies.append(
                    send(to_col.at[step, k - 1], from_col.at[step, k - 1], row, place)
                )
        for k, copy in enumerate(col_copies):
            copy.wait_recv()
            piece = piece + from_col[step, k]
        c_shard = c_shard - rate[2] * piece
        if not last:
            c_whole[step + 1, plane, core, col] = c_shard
            begun = gather_start(step + 1, c_whole.at[step + 1, plane, core, col])
        else:
            c_out[...] = c_shard
        a_full = a_full - rate[0] * total(a_slots, step + 1, sent_a)
        b_full = b_full - rate[1] * total(b_slots, step + 1, sent_b)
    back = lax.rem(n_cols - col, n_cols) * width_a
    a_out[...] = pltpu.roll(a_full, back, 1)[:n_i, :width_a]
    back = lax.rem(n_rows - row, n_rows) * width_b
    b_out[...] = pltpu.roll(b_full, back, 1)[:, :width_b]
    for copy in used:
        copy.wait_send()


def n_copies(n_rows, n_cols):
    half = n_rows // 2
    shares = (STEPS + 1) * (n_cols + n_rows - 2)
    gather = n_cols - 1 + n_cols * (half - 1) + n_cols * half
    scatter = half + (half - 1) * n_cols + n_cols - 1
    return shares + STEPS * (gather + scatter)


def per_device(tensor, first_factor, second_factor, third_factor):
    n_rows, n_cols = lax.axis_size("rows"), lax.axis_size("cols")
    count, rank = third_factor.shape
    n_i, n_j, depth = tensor.shape
    if count % 8 or n_rows % 2 or n_j % 16:
        return plain_steps(tensor, first_factor, second_factor, third_factor)
    half = n_rows // 2
    tall = -(-n_i // 8) * 8
    f32, bf16 = jnp.float32, jnp.bfloat16
    copies = n_copies(n_rows, n_cols)
    vmem = pl.BlockSpec(memory_space=pltpu.VMEM)
    return pl.pallas_call(
        functools.partial(kernel, n_rows, n_cols, rates(tensor)),
        out_shape=tuple(
            jax.ShapeDtypeStruct(x.shape, f32) for x in (first_factor, second_factor, third_factor)
        ),
        in_specs=[vmem] * 4,
        out_specs=(vmem,) * 3,
        scratch_shapes=[
            pltpu.VMEM((STEPS + 1, n_cols, tall, rank), f32),
            pltpu.VMEM((STEPS + 1, n_rows, n_j, rank), f32),
            pltpu.VMEM((STEPS, half, 2, n_cols, count, rank), f32),
            pltpu.VMEM((STEPS, half, 2, n_cols, count, rank), f32),
            pltpu.VMEM((STEPS, half, n_cols, count, rank), f32),
            pltpu.VMEM((STEPS, max(half - 1, 1), n_cols, count, rank), f32),
            pltpu.VMEM((STEPS, max(half - 1, 1), n_cols, count, rank), f32),
            pltpu.VMEM((STEPS, n_cols, count, rank), f32),
            pltpu.VMEM((STEPS, n_cols, count, rank), f32),
            pltpu.VMEM((n_i * n_j, rank), bf16),
            pltpu.VMEM((n_i * n_j, rank), bf16),
            pltpu.VMEM((n_i * n_j, depth), bf16),
            pltpu.VMEM((n_i * n_j, depth), bf16),
            pltpu.VMEM((tall, rank), f32),
            pltpu.VMEM((n_j, rank), f32),
            pltpu.SemaphoreType.DMA((copies,)),
            pltpu.SemaphoreType.DMA((copies,)),
        ],
        compiler_params=pltpu.CompilerParams(
            collective_id=0, has_side_effects=True, vmem_limit_bytes=48 << 20
        ),
    )(tensor.reshape(n_i * n_j, depth), first_factor, second_factor, third_factor)


def solution(mesh):
    in_specs = (
        P("rows", "cols", None),
        P("rows", "cols"),
        P("cols", "rows"),
        P(("rows", "cols"), None),
    )
    out_specs = (P("rows", "cols"), P("cols", "rows"), P(("rows", "cols"), None))
    return jax.shard_map(
        per_device, mesh=mesh, in_specs=in_specs, out_specs=out_specs, check_vma=False
    )
```

```python
import functools

import jax
import jax.numpy as jnp
from jax import lax
from jax.experimental import pallas as pl
from jax.experimental.pallas import tpu as pltpu
from jax.sharding import PartitionSpec as P

STEPS = 2
MESH = pl.DeviceIdType.MESH


def gather_third(piece):
    return lax.all_gather(piece, ("rows", "cols"), axis=0, tiled=True)


def plain_steps(tensor, first_factor, second_factor, third_factor):
    high = lax.Precision.HIGHEST
    rows_dev, cols_dev, depth = tensor.shape
    rate_a, rate_b, rate_c = rates(tensor)
    flat_target = tensor.reshape(-1, depth)
    shard_a, shard_b = (first_factor, second_factor)
    whole_c = gather_third(third_factor)
    for step_index in range(STEPS):
        whole_a = lax.all_gather(shard_a, "cols", axis=1, tiled=True)
        whole_b = lax.all_gather(shard_b, "rows", axis=1, tiled=True)
        khatri = (whole_a[:, None, :] * whole_b[None, :, :]).reshape(-1, whole_a.shape[1])
        model_tile = jnp.dot(khatri, whole_c.T, precision=high, preferred_element_type=jnp.float32)
        deriv = jax.nn.sigmoid(model_tile) - flat_target
        deriv_c = jnp.dot(
            deriv, whole_c, precision=high, preferred_element_type=jnp.float32
        ).reshape(rows_dev, cols_dev, -1)
        term_a = jnp.einsum("ijr,jr->ir", deriv_c, whole_b, precision=high)
        term_b = jnp.einsum("ijr,ir->jr", deriv_c, whole_a, precision=high)
        term_c = lax.dot_general(
            deriv, khatri, (((0,), (0,)), ((), ())), precision=high,
            preferred_element_type=jnp.float32,
        )
        shard_a = shard_a - rate_a * lax.psum_scatter(
            term_a, "cols", scatter_dimension=1, tiled=True
        )
        shard_b = shard_b - rate_b * lax.psum_scatter(
            term_b, "rows", scatter_dimension=1, tiled=True
        )
        whole_c = whole_c - rate_c * lax.psum(term_c, ("rows", "cols"))
    owner = lax.axis_index("rows") * lax.axis_size("cols") + lax.axis_index("cols")
    count = third_factor.shape[0]
    shard_c = lax.dynamic_slice_in_dim(whole_c, owner * count, count, 0)
    return (shard_a, shard_b, shard_c)


def rates(tensor):
    rows_dev, cols_dev, depth = tensor.shape
    size_i = rows_dev * lax.axis_size("rows")
    size_j = cols_dev * lax.axis_size("cols")
    return (
        4.0 / float(size_j * depth) ** 0.5,
        4.0 / float(size_i * depth) ** 0.5,
        4.0 / float(size_i * size_j) ** 0.5,
    )


def split(x):
    hi = x.astype(jnp.bfloat16)
    return hi, (x - hi.astype(jnp.float32)).astype(jnp.bfloat16)


def dot3(lhs, rhs, dims):
    def one(a, b):
        return lax.dot_general(a, b, (dims, ((), ())), preferred_element_type=jnp.float32)

    return one(lhs[0], rhs[0]) + (one(lhs[0], rhs[1]) + one(lhs[1], rhs[0]))


def kernel(
    n_rows, n_cols, rate, target_ref, a_ref, b_ref, c_ref, a_out, b_out, c_out,
    target, a_slots, a_rows, a_leave, a_arrive, b_slots, c_whole, c_leave, c_arrive,
    khatri_hi, khatri_lo, prob, place_a, place_b, own_sem, send_sem, recv_sem,
):
    half = n_rows // 2
    n_i, n_j = a_ref.shape[0], b_ref.shape[0]
    width_a, width_b = a_ref.shape[1], b_ref.shape[1]
    rank = c_ref.shape[1]
    depth = target.shape[2]
    row, col = lax.axis_index("rows"), lax.axis_index("cols")
    plane, core = lax.div(row, 2), lax.rem(row, 2)
    used = []

    def turn(base, offset, size):
        return lax.rem(base + offset, size)

    def send(src, dst, to_row, to_col):
        number = len(used)
        copy = pltpu.make_async_remote_copy(
            src_ref=src, dst_ref=dst, send_sem=send_sem.at[number], recv_sem=recv_sem.at[number],
            device_id=(to_row, to_col), device_id_type=MESH,
        )
        used.append(copy)
        copy.start()
        return copy

    steps_away = [(h, flip) for h in range(half) for flip in (0, 1)][1:]
    to_rows = [turn(plane, h, half) * 2 + lax.rem(core + flip, 2) for h, flip in steps_away]
    of_rows = [turn(plane, half - h, half) * 2 + lax.rem(core + flip, 2) for h, flip in steps_away]
    to_cols = [turn(col, k, n_cols) for k in range(1, n_cols)]

    own = pltpu.make_async_copy(
        target_ref.at[:, pl.ds(pl.multiple_of(row * depth, 128), depth)], target.at[row], own_sem.at[0]
    )
    own.start()
    barrier = pltpu.get_barrier_semaphore()
    for there in to_cols:
        pl.semaphore_signal(barrier, inc=1, device_id=(row, there), device_id_type=MESH)
    for there in to_rows:
        pl.semaphore_signal(barrier, inc=1, device_id=(there, col), device_id_type=MESH)
    pl.semaphore_wait(barrier, n_cols + n_rows - 2)

    def over_cols(src, dst):
        return [send(src, dst, row, there) for there in to_cols]

    def over_rows(src, dst):
        return [send(src, dst, there, col) for there in to_rows]

    def arrived(copies):
        for copy in copies:
            copy.wait_recv()

    def total(slots, version):
        result = slots[version, 0]
        for k in range(1, slots.shape[1]):
            result = result + slots[version, k]
        return result

    def share(slots, version, place, spread):
        return spread(slots.at[version, place], slots.at[version, place])

    sent_c = over_cols(c_ref, c_whole.at[0, col])
    place_a[...] = jnp.zeros_like(place_a)
    place_a[:n_i, :width_a] = a_ref[...]
    a_slots[0, col] = pltpu.roll(place_a[...], col * width_a, 1)
    sent_a = share(a_slots, 0, col, over_cols)
    place_b[...] = jnp.zeros_like(place_b)
    place_b[:, :width_b] = b_ref[...]
    b_slots[0, row] = pltpu.roll(place_b[...], row * width_b, 1)
    sent_b = share(b_slots, 0, row, over_rows)
    sent_target = [
        send(
            target_ref.at[:, pl.ds(pl.multiple_of(there * depth, 128), depth)],
            target.at[row], there, col,
        )
        for there in to_rows
    ]
    c_shard = c_ref[...]
    c_whole[0, col] = c_shard
    arrived(sent_a)
    a_own = total(a_slots, 0)
    a_rows[0, row] = a_own
    sent_rows = share(a_rows, 0, row, over_rows)
    arrived(sent_b)
    b_full = total(b_slots, 0)

    for step in range(STEPS):
        last = step == STEPS - 1
        blocks = [row] + of_rows
        for number, block in enumerate(blocks):
            if number:
                sent_rows[number - 1].wait_recv()
            a_block = a_rows[step, block]
            for i in range(n_i):
                hi, lo = split(a_block[i : i + 1, :] * b_full)
                khatri_hi[block, i * n_j : (i + 1) * n_j, :] = hi
                khatri_lo[block, i * n_j : (i + 1) * n_j, :] = lo
            if not number:
                arrived(sent_c)
                c_parts = split(c_whole[step].reshape(-1, rank))
            model = dot3((khatri_hi[block], khatri_lo[block]), c_parts, ((1,), (1,)))
            prob[block] = jax.nn.sigmoid(model)
        order = list(range(n_rows)) if step == 0 else list(range(1, n_rows)) + [0]
        term_c, term_b, term_own = None, None, None
        sent_terms = [None] * (n_rows - 1)
        for number in order:
            block = blocks[number]
            if step == 0:
                if number:
                    sent_target[number - 1].wait_recv()
                else:
                    own.wait()
            deriv = split(prob[block] - target[block])
            deriv_c = dot3(deriv, c_parts, ((1,), (0,))).reshape(n_i, n_j, rank)
            term_a = jnp.sum(deriv_c * b_full[None, :, :], axis=1)
            if number:
                a_leave[step, number - 1] = jnp.zeros_like(place_a)
                a_leave[step, number - 1, :n_i, :] = term_a
                sent_terms[number - 1] = send(
                    a_leave.at[step, number - 1], a_arrive.at[step, number - 1], block, col
                )
            else:
                term_own = term_a
            a_block = a_rows[step, block][:n_i, :]
            part_b = jnp.sum(deriv_c * a_block[:, None, :], axis=0)
            part_c = dot3(deriv, (khatri_hi[block], khatri_lo[block]), ((0,), (0,)))
            term_b = part_b if term_b is None else term_b + part_b
            term_c = part_c if term_c is None else term_c + part_c
        c_leave[step] = term_c.reshape(c_leave.shape[1:])
        sent_c = [
            send(c_leave.at[step, there], c_arrive.at[step, k], row, there)
            for k, there in enumerate(to_cols)
        ]
        b_slots[step + 1, row] = term_b
        sent_b = share(b_slots, step + 1, row, over_rows)
        place_a[...] = jnp.zeros_like(place_a)
        place_a[:n_i, :] = term_own
        arrived(sent_terms)
        term_own = place_a[...]
        for k in range(n_rows - 1):
            term_own = term_own + a_arrive[step, k]
        a_slots[step + 1, col] = term_own
        sent_a = share(a_slots, step + 1, col, over_cols)
        arrived(sent_c)
        grad_c = c_leave[step, col]
        for k in range(n_cols - 1):
            grad_c = grad_c + c_arrive[step, k]
        c_shard = c_shard - rate[2] * grad_c
        if last:
            c_out[...] = c_shard
        else:
            c_whole[step + 1, col] = c_shard
            sent_c = share(c_whole, step + 1, col, over_cols)
        arrived(sent_a)
        a_own = a_own - rate[0] * total(a_slots, step + 1)
        if not last:
            a_rows[step + 1, row] = a_own
            sent_rows = share(a_rows, step + 1, row, over_rows)
        arrived(sent_b)
        b_full = b_full - rate[1] * total(b_slots, step + 1)
    back = lax.rem(n_cols - col, n_cols) * width_a
    a_out[...] = pltpu.roll(a_own, back, 1)[:n_i, :width_a]
    back = lax.rem(n_rows - row, n_rows) * width_b
    b_out[...] = pltpu.roll(b_full, back, 1)[:, :width_b]
    for copy in used:
        copy.wait_send()


def n_copies(n_rows, n_cols):
    rows, cols = n_rows - 1, n_cols - 1
    return rows + (STEPS + 1) * (cols + rows) + STEPS * (rows + cols) + STEPS * (rows + cols)


def per_device(tensor, first_factor, second_factor, third_factor):
    n_rows, n_cols = lax.axis_size("rows"), lax.axis_size("cols")
    count, rank = third_factor.shape
    n_i, n_j, depth = tensor.shape
    part = depth // n_rows
    if count % 8 or n_rows % 2 or n_j % 16 or part % 128:
        return plain_steps(tensor, first_factor, second_factor, third_factor)
    tall = -(-n_i // 8) * 8
    f32, bf16 = jnp.float32, jnp.bfloat16
    copies = n_copies(n_rows, n_cols)
    vmem = pl.BlockSpec(memory_space=pltpu.VMEM)
    return pl.pallas_call(
        functools.partial(kernel, n_rows, n_cols, rates(tensor)),
        out_shape=tuple(
            jax.ShapeDtypeStruct(x.shape, f32) for x in (first_factor, second_factor, third_factor)
        ),
        in_specs=[pl.BlockSpec(memory_space=pltpu.HBM)] + [vmem] * 3,
        out_specs=(vmem,) * 3,
        scratch_shapes=[
            pltpu.VMEM((n_rows, n_i * n_j, part), f32),
            pltpu.VMEM((STEPS + 1, n_cols, tall, rank), f32),
            pltpu.VMEM((STEPS, n_rows, tall, rank), f32),
            pltpu.VMEM((STEPS, n_rows - 1, tall, rank), f32),
            pltpu.VMEM((STEPS, n_rows - 1, tall, rank), f32),
            pltpu.VMEM((STEPS + 1, n_rows, n_j, rank), f32),
            pltpu.VMEM((STEPS, n_cols, count, rank), f32),
            pltpu.VMEM((STEPS, n_cols, count, rank), f32),
            pltpu.VMEM((STEPS, n_cols - 1, count, rank), f32),
            pltpu.VMEM((n_rows, n_i * n_j, rank), bf16),
            pltpu.VMEM((n_rows, n_i * n_j, rank), bf16),
            pltpu.VMEM((n_rows, n_i * n_j, part), f32),
            pltpu.VMEM((tall, rank), f32),
            pltpu.VMEM((n_j, rank), f32),
            pltpu.SemaphoreType.DMA((1,)),
            pltpu.SemaphoreType.DMA((copies,)),
            pltpu.SemaphoreType.DMA((copies,)),
        ],
        compiler_params=pltpu.CompilerParams(
            collective_id=0, has_side_effects=True, vmem_limit_bytes=48 << 20
        ),
    )(tensor.reshape(n_i * n_j, depth), first_factor, second_factor, third_factor)


def solution(mesh):
    in_specs = (
        P("rows", "cols", None),
        P("rows", "cols"),
        P("cols", "rows"),
        P(("rows", "cols"), None),
    )
    out_specs = (P("rows", "cols"), P("cols", "rows"), P(("rows", "cols"), None))
    return jax.shard_map(
        per_device, mesh=mesh, in_specs=in_specs, out_specs=out_specs, check_vma=False
    )
```

```python
import functools

import jax
import jax.numpy as jnp
from jax import lax
from jax.experimental import pallas as pl
from jax.experimental.pallas import tpu as pltpu
from jax.sharding import PartitionSpec as P

STEPS = 2
MESH = pl.DeviceIdType.MESH


def gather_third(piece):
    return lax.all_gather(piece, ("rows", "cols"), axis=0, tiled=True)


def plain_steps(tensor, first_factor, second_factor, third_factor):
    high = lax.Precision.HIGHEST
    rows_dev, cols_dev, depth = tensor.shape
    rate_a, rate_b, rate_c = rates(tensor)
    flat_target = tensor.reshape(-1, depth)
    shard_a, shard_b = (first_factor, second_factor)
    whole_c = gather_third(third_factor)
    for step_index in range(STEPS):
        whole_a = lax.all_gather(shard_a, "cols", axis=1, tiled=True)
        whole_b = lax.all_gather(shard_b, "rows", axis=1, tiled=True)
        khatri = (whole_a[:, None, :] * whole_b[None, :, :]).reshape(-1, whole_a.shape[1])
        model_tile = jnp.dot(khatri, whole_c.T, precision=high, preferred_element_type=jnp.float32)
        deriv = jax.nn.sigmoid(model_tile) - flat_target
        deriv_c = jnp.dot(
            deriv, whole_c, precision=high, preferred_element_type=jnp.float32
        ).reshape(rows_dev, cols_dev, -1)
        term_a = jnp.einsum("ijr,jr->ir", deriv_c, whole_b, precision=high)
        term_b = jnp.einsum("ijr,ir->jr", deriv_c, whole_a, precision=high)
        term_c = lax.dot_general(
            deriv, khatri, (((0,), (0,)), ((), ())), precision=high,
            preferred_element_type=jnp.float32,
        )
        shard_a = shard_a - rate_a * lax.psum_scatter(
            term_a, "cols", scatter_dimension=1, tiled=True
        )
        shard_b = shard_b - rate_b * lax.psum_scatter(
            term_b, "rows", scatter_dimension=1, tiled=True
        )
        whole_c = whole_c - rate_c * lax.psum(term_c, ("rows", "cols"))
    owner = lax.axis_index("rows") * lax.axis_size("cols") + lax.axis_index("cols")
    count = third_factor.shape[0]
    shard_c = lax.dynamic_slice_in_dim(whole_c, owner * count, count, 0)
    return (shard_a, shard_b, shard_c)


def rates(tensor):
    rows_dev, cols_dev, depth = tensor.shape
    size_i = rows_dev * lax.axis_size("rows")
    size_j = cols_dev * lax.axis_size("cols")
    return (
        4.0 / float(size_j * depth) ** 0.5,
        4.0 / float(size_i * depth) ** 0.5,
        4.0 / float(size_i * size_j) ** 0.5,
    )


def split(x):
    hi = x.astype(jnp.bfloat16)
    return hi, (x - hi.astype(jnp.float32)).astype(jnp.bfloat16)


def dot3(lhs, rhs, dims):
    def one(a, b):
        return lax.dot_general(a, b, (dims, ((), ())), preferred_element_type=jnp.float32)

    return one(lhs[0], rhs[0]) + (one(lhs[0], rhs[1]) + one(lhs[1], rhs[0]))


def kernel(
    n_rows, n_cols, rate, target_ref, a_ref, b_ref, c_ref, a_out, b_out, c_out,
    target, a_slots, a_rows, a_leave, a_arrive, b_slots, c_whole, c_leave, c_arrive,
    khatri_hi, khatri_lo, prob, place_a, place_b, own_sem, send_sem, recv_sem,
):
    half = n_rows // 2
    n_i, n_j = a_ref.shape[0], b_ref.shape[0]
    width_a, width_b = a_ref.shape[1], b_ref.shape[1]
    rank = c_ref.shape[1]
    depth = target.shape[2]
    row, col = lax.axis_index("rows"), lax.axis_index("cols")
    plane, core = lax.div(row, 2), lax.rem(row, 2)
    used = []

    def turn(base, offset, size):
        return lax.rem(base + offset, size)

    def send(src, dst, to_row, to_col):
        number = len(used)
        copy = pltpu.make_async_remote_copy(
            src_ref=src, dst_ref=dst, send_sem=send_sem.at[number], recv_sem=recv_sem.at[number],
            device_id=(to_row, to_col), device_id_type=MESH,
        )
        used.append(copy)
        copy.start()
        return copy

    steps_away = [(h, flip) for h in range(half) for flip in (0, 1)][1:]
    to_rows = [turn(plane, h, half) * 2 + lax.rem(core + flip, 2) for h, flip in steps_away]
    of_rows = [turn(plane, half - h, half) * 2 + lax.rem(core + flip, 2) for h, flip in steps_away]
    to_cols = [turn(col, k, n_cols) for k in range(1, n_cols)]

    own = pltpu.make_async_copy(
        target_ref.at[:, pl.ds(pl.multiple_of(row * depth, 128), depth)], target.at[row], own_sem.at[0]
    )
    own.start()
    barrier = pltpu.get_barrier_semaphore()
    for there in to_cols:
        pl.semaphore_signal(barrier, inc=1, device_id=(row, there), device_id_type=MESH)
    for there in to_rows:
        pl.semaphore_signal(barrier, inc=1, device_id=(there, col), device_id_type=MESH)
    pl.semaphore_wait(barrier, n_cols + n_rows - 2)

    def over_cols(src, dst):
        return [send(src, dst, row, there) for there in to_cols]

    def over_rows(src, dst):
        return [send(src, dst, there, col) for there in to_rows]

    def arrived(copies):
        for copy in copies:
            copy.wait_recv()

    def total(slots, version):
        result = slots[version, 0]
        for k in range(1, slots.shape[1]):
            result = result + slots[version, k]
        return result

    def share(slots, version, place, spread):
        return spread(slots.at[version, place], slots.at[version, place])

    sent_c = over_cols(c_ref, c_whole.at[0, col])
    place_a[...] = jnp.zeros_like(place_a)
    place_a[:n_i, :width_a] = a_ref[...]
    a_slots[0, col] = pltpu.roll(place_a[...], col * width_a, 1)
    sent_a = share(a_slots, 0, col, over_cols)
    place_b[...] = jnp.zeros_like(place_b)
    place_b[:, :width_b] = b_ref[...]
    b_slots[0, row] = pltpu.roll(place_b[...], row * width_b, 1)
    sent_b = share(b_slots, 0, row, over_rows)
    sent_target = [
        send(
            target_ref.at[:, pl.ds(pl.multiple_of(there * depth, 128), depth)],
            target.at[row], there, col,
        )
        for there in to_rows
    ]
    c_shard = c_ref[...]
    c_whole[0, col] = c_shard
    arrived(sent_a)
    a_own = total(a_slots, 0)
    a_rows[0, row] = a_own
    sent_rows = share(a_rows, 0, row, over_rows)
    arrived(sent_b)
    b_full = total(b_slots, 0)

    for step in range(STEPS):
        last = step == STEPS - 1
        blocks = [row] + of_rows
        for number, block in enumerate(blocks):
            if number:
                sent_rows[number - 1].wait_recv()
            a_block = a_rows[step, block]
            for i in range(n_i):
                hi, lo = split(a_block[i : i + 1, :] * b_full)
                khatri_hi[block, i * n_j : (i + 1) * n_j, :] = hi
                khatri_lo[block, i * n_j : (i + 1) * n_j, :] = lo
            if not number:
                arrived(sent_c)
                c_parts = split(c_whole[step].reshape(-1, rank))
            model = dot3((khatri_hi[block], khatri_lo[block]), c_parts, ((1,), (1,)))
            prob[block] = jax.nn.sigmoid(model)
        order = list(range(n_rows)) if step == 0 else list(range(1, n_rows)) + [0]
        term_c, term_b, term_own = None, None, None
        sent_terms = [None] * (n_rows - 1)
        derivs = {}
        for number in order:
            block = blocks[number]
            if step == 0:
                if number:
                    sent_target[number - 1].wait_recv()
                else:
                    own.wait()
            derivs[number] = split(prob[block] - target[block])
            part_c = dot3(derivs[number], (khatri_hi[block], khatri_lo[block]), ((0,), (0,)))
            term_c = part_c if term_c is None else term_c + part_c
        c_leave[step] = term_c.reshape(c_leave.shape[1:])
        sent_c = [
            send(c_leave.at[step, there], c_arrive.at[step, k], row, there)
            for k, there in enumerate(to_cols)
        ]
        for number in list(range(1, n_rows)) + [0]:
            block = blocks[number]
            deriv_c = dot3(derivs[number], c_parts, ((1,), (0,))).reshape(n_i, n_j, rank)
            term_a = jnp.sum(deriv_c * b_full[None, :, :], axis=1)
            if number:
                a_leave[step, number - 1] = jnp.zeros_like(place_a)
                a_leave[step, number - 1, :n_i, :] = term_a
                sent_terms[number - 1] = send(
                    a_leave.at[step, number - 1], a_arrive.at[step, number - 1], block, col
                )
            else:
                term_own = term_a
            a_block = a_rows[step, block][:n_i, :]
            part_b = jnp.sum(deriv_c * a_block[:, None, :], axis=0)
            term_b = part_b if term_b is None else term_b + part_b
        b_slots[step + 1, row] = term_b
        sent_b = share(b_slots, step + 1, row, over_rows)
        place_a[...] = jnp.zeros_like(place_a)
        place_a[:n_i, :] = term_own
        arrived(sent_terms)
        term_own = place_a[...]
        for k in range(n_rows - 1):
            term_own = term_own + a_arrive[step, k]
        a_slots[step + 1, col] = term_own
        sent_a = share(a_slots, step + 1, col, over_cols)
        arrived(sent_c)
        grad_c = c_leave[step, col]
        for k in range(n_cols - 1):
            grad_c = grad_c + c_arrive[step, k]
        c_shard = c_shard - rate[2] * grad_c
        if last:
            c_out[...] = c_shard
        else:
            c_whole[step + 1, col] = c_shard
            sent_c = share(c_whole, step + 1, col, over_cols)
        arrived(sent_a)
        a_own = a_own - rate[0] * total(a_slots, step + 1)
        if not last:
            a_rows[step + 1, row] = a_own
            sent_rows = share(a_rows, step + 1, row, over_rows)
        arrived(sent_b)
        b_full = b_full - rate[1] * total(b_slots, step + 1)
    back = lax.rem(n_cols - col, n_cols) * width_a
    a_out[...] = pltpu.roll(a_own, back, 1)[:n_i, :width_a]
    back = lax.rem(n_rows - row, n_rows) * width_b
    b_out[...] = pltpu.roll(b_full, back, 1)[:, :width_b]
    for copy in used:
        copy.wait_send()


def n_copies(n_rows, n_cols):
    rows, cols = n_rows - 1, n_cols - 1
    return rows + (STEPS + 1) * (cols + rows) + STEPS * (rows + cols) + STEPS * (rows + cols)


def per_device(tensor, first_factor, second_factor, third_factor):
    n_rows, n_cols = lax.axis_size("rows"), lax.axis_size("cols")
    count, rank = third_factor.shape
    n_i, n_j, depth = tensor.shape
    part = depth // n_rows
    if count % 8 or n_rows % 2 or n_j % 16 or part % 128:
        return plain_steps(tensor, first_factor, second_factor, third_factor)
    tall = -(-n_i // 8) * 8
    f32, bf16 = jnp.float32, jnp.bfloat16
    copies = n_copies(n_rows, n_cols)
    vmem = pl.BlockSpec(memory_space=pltpu.VMEM)
    return pl.pallas_call(
        functools.partial(kernel, n_rows, n_cols, rates(tensor)),
        out_shape=tuple(
            jax.ShapeDtypeStruct(x.shape, f32) for x in (first_factor, second_factor, third_factor)
        ),
        in_specs=[pl.BlockSpec(memory_space=pltpu.HBM)] + [vmem] * 3,
        out_specs=(vmem,) * 3,
        scratch_shapes=[
            pltpu.VMEM((n_rows, n_i * n_j, part), f32),
            pltpu.VMEM((STEPS + 1, n_cols, tall, rank), f32),
            pltpu.VMEM((STEPS, n_rows, tall, rank), f32),
            pltpu.VMEM((STEPS, n_rows - 1, tall, rank), f32),
            pltpu.VMEM((STEPS, n_rows - 1, tall, rank), f32),
            pltpu.VMEM((STEPS + 1, n_rows, n_j, rank), f32),
            pltpu.VMEM((STEPS, n_cols, count, rank), f32),
            pltpu.VMEM((STEPS, n_cols, count, rank), f32),
            pltpu.VMEM((STEPS, n_cols - 1, count, rank), f32),
            pltpu.VMEM((n_rows, n_i * n_j, rank), bf16),
            pltpu.VMEM((n_rows, n_i * n_j, rank), bf16),
            pltpu.VMEM((n_rows, n_i * n_j, part), f32),
            pltpu.VMEM((tall, rank), f32),
            pltpu.VMEM((n_j, rank), f32),
            pltpu.SemaphoreType.DMA((1,)),
            pltpu.SemaphoreType.DMA((copies,)),
            pltpu.SemaphoreType.DMA((copies,)),
        ],
        compiler_params=pltpu.CompilerParams(
            collective_id=0, has_side_effects=True, vmem_limit_bytes=48 << 20
        ),
    )(tensor.reshape(n_i * n_j, depth), first_factor, second_factor, third_factor)


def solution(mesh):
    in_specs = (
        P("rows", "cols", None),
        P("rows", "cols"),
        P("cols", "rows"),
        P(("rows", "cols"), None),
    )
    out_specs = (P("rows", "cols"), P("cols", "rows"), P(("rows", "cols"), None))
    return jax.shard_map(
        per_device, mesh=mesh, in_specs=in_specs, out_specs=out_specs, check_vma=False
    )
```
